128 devices in a mesh: srow: 16 (over x, z), scol: 4 (over y_hi, core), trow: 2 (over y_lo).
Axes of the slice: x: 4, y: 4 (y_hi: 2, y_lo: 2; y = y_hi * 2 + y_lo), z: 4, core: 2. Of those that a mesh axis runs over, the one named last changes fastest.
Arguments:
- volume: bfloat16 [8, 32, 16, 128, 128], P(None, 'srow', 'scol', 'trow'), may hold values from -6 to 6
- src_weight: bfloat16 [2, 9, 8, 8], replicated, may hold values from -0.75 to 0.75
- tgt_weight: bfloat16 [2, 9, 8, 8], replicated, may hold values from -0.75 to 0.75
- bias: float32 [2, 8], replicated, may hold values from -3 to 3
Outputs:
- refined: bfloat16 [8, 32, 16, 128, 128], P(None, 'srow', 'scol', 'trow')
The draws below stay inside these ranges and needn't reach their ends.
All inputs are finite; a program needn't handle non-finite values.
Results may differ from the reference program's by a relative error of at most 0.0036.
Values may be sent and summed in bfloat16 or wider, within the bound.
A program may use at most 64 MiB of HBM per device.

```python
import jax
import jax.numpy as jnp
from jax import lax

C = 8
TC = 128
LAYERS = 2
NI = 32
NJ = 16
NK = 128


def levels(own_key, extent, cuts, smallest, top_value):
    gain, own = 1.0, jax.random.fold_in(own_key, 6)
    for dim, shards_of in cuts:
        steps = jnp.exp(jax.random.uniform(jax.random.fold_in(own, dim), (shards_of,), jnp.float32, smallest / len(cuts), top_value / len(cuts)))
        gain = gain * jnp.repeat(steps, extent[dim] // shards_of).reshape([-1 if axis == dim else 1 for axis in range(len(extent))])
    return gain


def centred(stream_key, extent, deviation, reach, cuts=(), held_as=jnp.bfloat16):
    array = deviation * jax.random.normal(stream_key, extent, jnp.float32)
    if cuts:
        array = array * levels(stream_key, extent, cuts, -0.22, 0.18)
    return jnp.clip(array, -reach, reach).astype(held_as)


def setup_inputs(seed: int = 0) -> dict:
    key_of = jax.random.split(jax.random.key(seed), 5)
    volume = centred(key_of[0], (C, NI, NJ, NK, TC), 1.0, 6.0, ((1, 16), (2, 4), (3, 2)))
    src_weight = centred(key_of[1], (LAYERS, 9, C, C), (9 * C) ** -0.5, 0.75)
    tgt_weight = centred(key_of[2], (LAYERS, 9, C, C), (9 * C) ** -0.5, 0.75)
    bias = centred(key_of[3], (LAYERS, C), 0.5, 3.0, (), jnp.float32)
    return dict(volume=volume, src_weight=src_weight, tgt_weight=tgt_weight, bias=bias)


def apply_layer(src_pad, tgt_pad, w_src, w_tgt, bias_row):
    source = src_pad.astype(jnp.float32)
    target = tgt_pad.astype(jnp.float32)
    channels, rows_two, cols_two, depth, width = source.shape
    row_count = rows_two - 2
    col_count = cols_two - 2
    widened = jnp.pad(target, ((0, 0), (0, 0), (0, 0), (0, 0), (1, 1)))
    total = jnp.zeros((channels, row_count, col_count, depth, width), jnp.float32)
    for first in range(3):
        for second in range(3):
            piece = source[:, first:first + row_count, second:second + col_count]
            kernel = w_src[3 * first + second].astype(jnp.float32)
            total = total + jnp.einsum("oc,cijkl->oijkl", kernel, piece, precision=lax.Precision.HIGHEST)
    for first in range(3):
        for second in range(3):
            piece = widened[:, :, :, first:first + depth, second:second + width]
            kernel = w_tgt[3 * first + second].astype(jnp.float32)
            total = total + jnp.einsum("oc,cijkl->oijkl", kernel, piece, precision=lax.Precision.HIGHEST)
    center = target[:, :, :, 1:1 + depth]
    return center + jnp.maximum(total + bias_row[:, None, None, None, None], 0.0)


def reference(volume, src_weight, tgt_weight, bias):
    state = volume
    for layer_id in range(LAYERS):
        src_pad = jnp.pad(state, ((0, 0), (1, 1), (1, 1), (0, 0), (0, 0)))
        tgt_pad = jnp.pad(state, ((0, 0), (0, 0), (0, 0), (1, 1), (0, 0)))
        state = apply_layer(src_pad, tgt_pad, src_weight[layer_id], tgt_weight[layer_id], bias[layer_id]).astype(jnp.bfloat16)
    return state
```

```python
import functools

import jax
import jax.numpy as jnp
from jax import lax
from jax.experimental import pallas as pl
from jax.experimental.pallas import tpu as pltpu
from jax.sharding import PartitionSpec as P

MESH = pl.DeviceIdType.MESH
BF16 = jnp.bfloat16
F32 = jnp.float32
STEP = 16
PAD = 8


def iota(shape, dim):
    return lax.broadcasted_iota(jnp.int32, shape, dim)


def expand(rows_of, taps):
    spread = (iota((8, 128), 1) // STEP == iota((8, 128), 0)).astype(BF16)
    wide = jnp.dot(taps, spread, preferred_element_type=F32)
    wide = jnp.concatenate([wide[8 * tap : 8 * tap + 8] for tap in range(9)], axis=1)
    return jnp.dot(rows_of, wide.astype(BF16), preferred_element_type=F32)


def build_weights(layer, ws_ref, wt_ref, src_mat, tgt_mat):
    rows = (iota((128, 8), 0) // STEP == iota((128, 8), 1)).astype(BF16)
    edge_rows = (iota((64, 8), 0) // 8 == iota((64, 8), 1)).astype(BF16)
    row, col = iota((128, 128), 0) % STEP, iota((128, 128), 1) % STEP
    zero = jnp.zeros((128, 128), F32)
    src = expand(rows, ws_ref[pl.ds(72 * layer, 72), :])
    for first in range(3):
        for second in range(3):
            tap = 3 * first + second
            block = jnp.where(row == col, src[:, 128 * tap : 128 * tap + 128], zero).astype(BF16)
            for i in range(2):
                place = 128 * (3 * (first + i) + second)
                src_mat[layer, 128 * i : 128 * i + 128, place : place + 128] = block
    for second in range(3):
        for i in range(2):
            place = 128 * (3 * (3 - 3 * i) + second)
            src_mat[layer, 128 * i : 128 * i + 128, place : place + 128] = zero.astype(BF16)
    taps = wt_ref[pl.ds(72 * layer, 72), :]
    own = expand(rows, taps)
    edge = expand(edge_rows, taps)
    edge_row, edge_col = iota((64, 128), 0) % 8, iota((64, 128), 1) % STEP
    up = (edge_row == 0) & (edge_col == STEP - 1)
    down = (edge_row == 7) & (edge_col == 0)
    for second in range(3):
        part = [slice(128 * (3 * first + second), 128 * (3 * first + second) + 128) for first in range(3)]
        block = jnp.where(col == row - 1, own[:, part[0]], zero)
        block = block + jnp.where(col == row, own[:, part[1]], zero)
        block = block + jnp.where(col == row + 1, own[:, part[2]], zero)
        place = slice(128 * second, 128 * second + 128)
        tgt_mat[layer, 0:128, place] = block.astype(BF16)
        tgt_mat[layer, 128:192, place] = jnp.where(up, edge[:, part[0]], 0.0).astype(BF16)
        tgt_mat[layer, 192:256, place] = jnp.where(down, edge[:, part[2]], 0.0).astype(BF16)


def kernel(
    sizes, x_ref, ws_ref, wt_ref, bias_ref, out_ref,
    buf0, buf1, sums0, sums1, src_mat, tgt_mat, edge_out, edge_in, staged,
    z_send, z_recv, j_send, j_recv, c_send, c_recv, e_send, e_recv, in_sem, out_sem,
):
    n_row, n_col = sizes
    channels, rows, cols, depth, width = x_ref.shape
    chunks = depth // STEP
    bufs, sums = (buf0, buf1), (sums0, sums1)
    r, s, t = lax.axis_index("srow"), lax.axis_index("scol"), lax.axis_index("trow")
    up, down = {"srow": lax.rem(r + 1, n_row)}, {"srow": lax.rem(r + n_row - 1, n_row)}
    right, left = {"scol": lax.rem(s + 1, n_col)}, {"scol": lax.rem(s + n_col - 1, n_col)}
    across = {"trow": 1 - t}
    has_up, has_down = r < n_row - 1, r > 0
    has_right, has_left = s < n_col - 1, s > 0

    def rows_of(block):
        return pl.ds(pl.multiple_of(block * STEP, STEP), STEP)

    def order(step):
        return (chunks - 1 - step) + t * (2 * step - (chunks - 1))

    def z_copy(layer, side, block):
        ks = rows_of(block)
        if layer == 0:
            src = x_ref.at[:, 0 if side == 0 else rows - 1, :, ks]
        else:
            src = buf1.at[:, 1 if side == 0 else rows, 1 : cols + 1, ks]
        return pltpu.make_async_remote_copy(
            src_ref=src,
            dst_ref=bufs[layer].at[:, rows + 1 if side == 0 else 0, 1 : cols + 1, ks],
            send_sem=z_send.at[layer, side, block],
            recv_sem=z_recv.at[layer, side, block],
            device_id=down if side == 0 else up,
            device_id_type=MESH,
        )

    def j_copy(layer, side, block):
        ks = rows_of(block)
        if layer == 0:
            src = x_ref.at[:, :, 0 if side == 0 else cols - 1, ks]
        else:
            src = buf1.at[:, 1 : rows + 1, 1 if side == 0 else cols, ks]
        return pltpu.make_async_remote_copy(
            src_ref=src,
            dst_ref=bufs[layer].at[:, 1 : rows + 1, cols + 1 if side == 0 else 0, ks],
            send_sem=j_send.at[layer, side, block],
            recv_sem=j_recv.at[layer, side, block],
            device_id=left if side == 0 else right,
            device_id_type=MESH,
        )

    def c_copy(layer, side, end, block):
        ks = rows_of(block)
        row = 0 if end == 0 else rows + 1
        return pltpu.make_async_remote_copy(
            src_ref=bufs[layer].at[:, row, 1 if side == 0 else cols, ks],
            dst_ref=bufs[layer].at[:, row, cols + 1 if side == 0 else 0, ks],
            send_sem=c_send.at[layer, side, end, block],
            recv_sem=c_recv.at[layer, side, end, block],
            device_id=left if side == 0 else right,
            device_id_type=MESH,
        )

    def e_copy(layer):
        return pltpu.make_async_remote_copy(
            src_ref=edge_out.at[layer],
            dst_ref=edge_in.at[layer],
            send_sem=e_send.at[layer],
            recv_sem=e_recv.at[layer],
            device_id=across,
            device_id_type=MESH,
        )

    z_sides = ((0, has_down, has_up), (1, has_up, has_down))
    j_sides = ((0, has_left, has_right), (1, has_right, has_left))
    ends = ((0, has_down), (1, has_up))

    barrier = pltpu.get_barrier_semaphore()
    for present, device in (
        (has_up, up), (has_down, down), (has_right, right), (has_left, left),
    ):
        @pl.when(present)
        def _():
            pl.semaphore_signal(barrier, inc=1, device_id=device, device_id_type=MESH)

    pl.semaphore_signal(barrier, inc=1, device_id=across, device_id_type=MESH)
    peers = 1 + sum(p.astype(jnp.int32) for p in (has_up, has_down, has_right, has_left))
    pl.semaphore_wait(barrier, peers)

    def send_chunk(layer, block):
        for side, sends, _ in z_sides:
            @pl.when(sends)
            def _():
                z_copy(layer, side, block).start()

        for side, sends, _ in j_sides:
            @pl.when(sends)
            def _():
                j_copy(layer, side, block).start()

    @pl.loop(0, chunks)
    def _(step):
        send_chunk(0, order(step))

    local = pltpu.make_async_copy(x_ref, buf0.at[:, 1 : rows + 1, 1 : cols + 1], in_sem)
    local.start()

    for buf in bufs:
        for row, present in ((0, has_down), (rows + 1, has_up)):
            @pl.when(jnp.logical_not(present))
            def _():
                buf[:, row] = jnp.zeros((channels, cols + 2, depth, width), BF16)

        for col, present in ((0, has_left), (cols + 1, has_right)):
            @pl.when(jnp.logical_not(present))
            def _():
                buf[:, :, col] = jnp.zeros((channels, rows + 2, depth, width), BF16)

    for layer in range(2):
        build_weights(layer, ws_ref, wt_ref, src_mat, tgt_mat)
        spare = jnp.zeros((channels, rows, cols, PAD, width), F32)
        sums[layer][:, :, :, 0:PAD] = spare
        sums[layer][:, :, :, depth + PAD : depth + 2 * PAD] = spare
        for channel in range(channels):
            sums[layer][channel, :, :, PAD : depth + PAD] = jnp.full(
                (rows, cols, depth, width), bias_ref[layer, channel], F32
            )

    lane = iota((channels * STEP, width), 1)

    def target_pass(layer, block):
        buf, total = bufs[layer], sums[layer]
        ks = rows_of(block)
        base = pl.multiple_of(block * STEP, STEP)
        for i in range(rows):
            for pair in range(cols // 2):
                shifted = [[], [], []]
                for n in range(2):
                    tile = buf[:, i + 1, 1 + 2 * pair + n, ks].reshape(channels * STEP, width)
                    wide = tile.astype(F32)
                    before = jnp.where(lane == 0, 0.0, pltpu.roll(wide, 1, 1))
                    after = jnp.where(lane == width - 1, 0.0, pltpu.roll(wide, width - 1, 1))
                    for second, piece in enumerate((before.astype(BF16), tile, after.astype(BF16))):
                        shifted[second].append(piece)
                stack = jnp.concatenate([jnp.concatenate(p, axis=1) for p in shifted], axis=0)
                got = jnp.dot(tgt_mat[layer], stack, preferred_element_type=F32)
                for n in range(2):
                    j = 2 * pair + n
                    part = got[:, width * n : width * n + width]
                    total[:, i, j, pl.ds(base + PAD, STEP)] += part[0:128].reshape(channels, STEP, width)
                    total[:, i, j, pl.ds(base + PAD + STEP, PAD)] += part[128:192].reshape(channels, PAD, width)
                    total[:, i, j, pl.ds(base, PAD)] += part[192:256].reshape(channels, PAD, width)

    def edge_start(layer):
        for half, place in ((0, depth + PAD), (1, PAD - 1)):
            @pl.when(t == half)
            def _():
                for i in range(rows):
                    for j in range(cols):
                        edge_out[layer, i, j] = sums[layer][:, i, j, place]

        e_copy(layer).start()

    def edge_add(layer):
        e_copy(layer).wait_recv()
        for half, place in ((0, depth + PAD - 1), (1, PAD)):
            @pl.when(t == half)
            def _():
                for i in range(rows):
                    for j in range(cols):
                        sums[layer][:, i, j, place] += edge_in[layer, i, j]

    def finish(layer, block):
        buf = bufs[layer]
        ks = rows_of(block)
        base = pl.multiple_of(block * STEP, STEP)
        for pair in range(cols // 2):
            tiles = [
                [buf[:, a, 2 * pair + b, ks].reshape(channels * STEP, width) for b in range(4)]
                for a in range(rows + 2)
            ]
            stack = jnp.concatenate(
                [
                    jnp.concatenate([tiles[a][b], tiles[a][b + 1]], axis=1)
                    for a in range(rows + 2)
                    for b in range(3)
                ],
                axis=0,
            )
            got = jnp.dot(src_mat[layer], stack, preferred_element_type=F32)
            for i in range(rows):
                for n in range(2):
                    j = 2 * pair + n
                    part = got[128 * i : 128 * i + 128, width * n : width * n + width]
                    part = part.reshape(channels, STEP, width)
                    part = part + sums[layer][:, i, j, pl.ds(base + PAD, STEP)]
                    center = tiles[i + 1][n + 1].reshape(channels, STEP, width).astype(F32)
                    value = (center + jnp.maximum(part, 0.0)).astype(BF16)
                    if layer == 0:
                        buf1[:, i + 1, j + 1, ks] = value
                    else:
                        staged[:, i, j, ks] = value

    def out_copy(block):
        ks = rows_of(block)
        return pltpu.make_async_copy(
            staged.at[:, :, :, ks], out_ref.at[:, :, :, ks], out_sem.at[block]
        )

    local.wait()

    @pl.loop(0, chunks)
    def _(step):
        target_pass(0, order(step))

        @pl.when(step == 0)
        def _():
            edge_start(0)

    for layer in range(2):
        @pl.loop(0, chunks + 1)
        def _(step):
            @pl.when(step < chunks)
            def _():
                block = order(step)
                for end, present in ends:
                    @pl.when(present)
                    def _():
                        z_copy(layer, 1 - end, block).wait_recv()
                        for side, sends, _ in j_sides:
                            @pl.when(sends)
                            def _():
                                c_copy(layer, side, end, block).start()

            @pl.when(step == 1)
            def _():
                edge_add(layer)

            @pl.when(step >= 1)
            def _():
                block = order(step - 1)
                for side, _, receives in j_sides:
                    @pl.when(receives)
                    def _():
                        j_copy(layer, side, block).wait_recv()

                    for end, present in ends:
                        @pl.when(receives & present)
                        def _():
                            c_copy(layer, side, end, block).wait_recv()

                finish(layer, block)
                if layer == 0:
                    send_chunk(1, block)
                    target_pass(1, block)

                    @pl.when(step == 1)
                    def _():
                        edge_start(1)
                else:
                    out_copy(block).start()

    @pl.loop(0, chunks)
    def _(block):
        for layer in range(2):
            for side, sends, _ in z_sides:
                @pl.when(sends)
                def _():
                    z_copy(layer, side, block).wait_send()

            for side, sends, _ in j_sides:
                @pl.when(sends)
                def _():
                    j_copy(layer, side, block).wait_send()

                for end, present in ends:
                    @pl.when(sends & present)
                    def _():
                        c_copy(layer, side, end, block).wait_send()

        out_copy(block).wait()

    for layer in range(2):
        e_copy(layer).wait_send()


def shards(sizes, volume, src_weight, tgt_weight, bias):
    channels, rows, cols, depth, width = volume.shape
    chunks = depth // STEP
    padded = pltpu.VMEM((channels, rows + 2, cols + 2, depth, width), BF16)
    total = pltpu.VMEM((channels, rows, cols, depth + 2 * PAD, width), F32)
    edges = pltpu.VMEM((2, rows, cols, channels, width), F32)
    dma = pltpu.SemaphoreType.DMA
    return pl.pallas_call(
        functools.partial(kernel, sizes),
        out_shape=jax.ShapeDtypeStruct(volume.shape, BF16),
        in_specs=[
            pl.BlockSpec(memory_space=pl.ANY),
            pl.BlockSpec(memory_space=pltpu.VMEM),
            pl.BlockSpec(memory_space=pltpu.VMEM),
            pl.BlockSpec(memory_space=pltpu.SMEM),
        ],
        out_specs=pl.BlockSpec(memory_space=pl.ANY),
        scratch_shapes=[
            padded, padded, total, total,
            pltpu.VMEM((2, 256, 12 * 128), BF16),
            pltpu.VMEM((2, 256, 3 * 128), BF16),
            edges, edges,
            pltpu.VMEM(volume.shape, BF16),
            dma((2, 2, chunks)), dma((2, 2, chunks)),
            dma((2, 2, chunks)), dma((2, 2, chunks)),
            dma((2, 2, 2, chunks)), dma((2, 2, 2, chunks)),
            dma((2,)), dma((2,)),
            dma, dma((chunks,)),
        ],
        compiler_params=pltpu.CompilerParams(
            collective_id=0, has_side_effects=True, vmem_limit_bytes=40 * 1024 * 1024
        ),
    )(volume, src_weight.reshape(-1, channels), tgt_weight.reshape(-1, channels), bias)


def solution(mesh):
    sizes = (mesh.shape["srow"], mesh.shape["scol"])
    return jax.shard_map(
        functools.partial(shards, sizes),
        mesh=mesh,
        in_specs=(P(None, "srow", "scol", "trow", None), P(), P(), P()),
        out_specs=P(None, "srow", "scol", "trow", None),
        check_vma=False,
    )
```

```python
import functools

import jax
import jax.numpy as jnp
from jax import lax
from jax.experimental import pallas as pl
from jax.experimental.pallas import tpu as pltpu
from jax.sharding import PartitionSpec as P

MESH = pl.DeviceIdType.MESH
BF16 = jnp.bfloat16
F32 = jnp.float32
STEP = 16
LEAD = 2
PAD = 8


def iota(shape, dim):
    return lax.broadcasted_iota(jnp.int32, shape, dim)


def expand(rows, taps):
    mine = iota((64, 128), 1) // STEP == iota((64, 128), 0) % 8
    wide = [jnp.where(mine, jnp.broadcast_to(taps[:, tap : tap + 1], (64, 128)), 0.0) for tap in range(9)]
    share = rows // 8
    spread = (iota((rows, 64), 0) // share == iota((rows, 64), 1) // 8).astype(BF16)
    wide = jnp.concatenate(wide, axis=1).astype(BF16)
    return jnp.dot(spread, wide, preferred_element_type=F32)


def build_weights(layer, ws_ref, wt_ref, src_mat, tgt_mat):
    row, col = iota((128, 128), 0) % STEP, iota((128, 128), 1) % STEP
    zero = jnp.zeros((128, 128), F32)
    src = expand(128, ws_ref[pl.ds(64 * layer, 64), :].astype(F32))
    for first in range(3):
        for second in range(3):
            tap = 3 * first + second
            block = jnp.where(row == col, src[:, 128 * tap : 128 * tap + 128], zero).astype(BF16)
            for i in range(2):
                place = 128 * (3 * (first + i) + second)
                src_mat[layer, 128 * i : 128 * i + 128, place : place + 128] = block
    for second in range(3):
        for i in range(2):
            place = 128 * (3 * (3 - 3 * i) + second)
            src_mat[layer, 128 * i : 128 * i + 128, place : place + 128] = zero.astype(BF16)
    taps = wt_ref[pl.ds(64 * layer, 64), :].astype(F32)
    own = expand(128, taps)
    edge = expand(64, taps)
    edge_row, edge_col = iota((64, 128), 0) % 8, iota((64, 128), 1) % STEP
    up = (edge_row == 0) & (edge_col == STEP - 1)
    down = (edge_row == 7) & (edge_col == 0)
    for second in range(3):
        part = [slice(128 * (3 * first + second), 128 * (3 * first + second) + 128) for first in range(3)]
        block = jnp.where(col == row - 1, own[:, part[0]], zero)
        block = block + jnp.where(col == row, own[:, part[1]], zero)
        block = block + jnp.where(col == row + 1, own[:, part[2]], zero)
        place = slice(128 * second, 128 * second + 128)
        tgt_mat[layer, 0:128, place] = block.astype(BF16)
        tgt_mat[layer, 128:192, place] = jnp.where(up, edge[:, part[0]], 0.0).astype(BF16)
        tgt_mat[layer, 192:256, place] = jnp.where(down, edge[:, part[2]], 0.0).astype(BF16)


def kernel(
    sizes, x_ref, ws_hbm, wt_hbm, bias_hbm, out_ref,
    ws_ref, wt_ref, bias_ref,
    buf0, buf1, sums0, sums1, src_mat, tgt_mat, edge_out, edge_in, staged,
    z_send, z_recv, j_send, j_recv, c_send, c_recv, e_send, e_recv, in_sem, out_sem,
):
    n_row, n_col = sizes
    channels, rows, cols, depth, width = x_ref.shape
    chunks = depth // STEP
    bufs, sums = (buf0, buf1), (sums0, sums1)
    r, s, t = lax.axis_index("srow"), lax.axis_index("scol"), lax.axis_index("trow")
    up, down = {"srow": lax.rem(r + 1, n_row)}, {"srow": lax.rem(r + n_row - 1, n_row)}
    right, left = {"scol": lax.rem(s + 1, n_col)}, {"scol": lax.rem(s + n_col - 1, n_col)}
    across = {"trow": 1 - t}
    has_up, has_down = r < n_row - 1, r > 0
    has_right, has_left = s < n_col - 1, s > 0

    def rows_of(block):
        return pl.ds(pl.multiple_of(block * STEP, STEP), STEP)

    def order(step):
        return (chunks - 1 - step) + t * (2 * step - (chunks - 1))

    def z_copy(layer, side, part, block):
        ks = rows_of(block)
        lo, hi = ((1, 2), (cols, cols + 1), (2, cols))[part]
        if layer == 0:
            src = x_ref.at[:, 0 if side == 0 else rows - 1, lo - 1 : hi - 1, ks]
        else:
            src = buf1.at[:, 1 if side == 0 else rows, lo:hi, ks]
        return pltpu.make_async_remote_copy(
            src_ref=src,
            dst_ref=bufs[layer].at[:, rows + 1 if side == 0 else 0, lo:hi, ks],
            send_sem=z_send.at[layer, side, part, block],
            recv_sem=z_recv.at[layer, side, part, block],
            device_id=down if side == 0 else up,
            device_id_type=MESH,
        )

    def j_copy(layer, side, block):
        ks = rows_of(block)
        if layer == 0:
            src = x_ref.at[:, :, 0 if side == 0 else cols - 1, ks]
        else:
            src = buf1.at[:, 1 : rows + 1, 1 if side == 0 else cols, ks]
        return pltpu.make_async_remote_copy(
            src_ref=src,
            dst_ref=bufs[layer].at[:, 1 : rows + 1, cols + 1 if side == 0 else 0, ks],
            send_sem=j_send.at[layer, side, block],
            recv_sem=j_recv.at[layer, side, block],
            device_id=left if side == 0 else right,
            device_id_type=MESH,
        )

    def c_copy(layer, side, end, block):
        ks = rows_of(block)
        row = 0 if end == 0 else rows + 1
        return pltpu.make_async_remote_copy(
            src_ref=bufs[layer].at[:, row, 1 if side == 0 else cols, ks],
            dst_ref=bufs[layer].at[:, row, cols + 1 if side == 0 else 0, ks],
            send_sem=c_send.at[layer, side, end, block],
            recv_sem=c_recv.at[layer, side, end, block],
            device_id=left if side == 0 else right,
            device_id_type=MESH,
        )

    def e_copy(layer):
        return pltpu.make_async_remote_copy(
            src_ref=edge_out.at[layer],
            dst_ref=edge_in.at[layer],
            send_sem=e_send.at[layer],
            recv_sem=e_recv.at[layer],
            device_id=across,
            device_id_type=MESH,
        )

    z_sides = ((0, has_down, has_up), (1, has_up, has_down))
    j_sides = ((0, has_left, has_right), (1, has_right, has_left))
    ends = ((0, has_down), (1, has_up))

    barrier = pltpu.get_barrier_semaphore()
    for present, device in (
        (has_up, up), (has_down, down), (has_right, right), (has_left, left),
    ):
        @pl.when(present)
        def _():
            pl.semaphore_signal(barrier, inc=1, device_id=device, device_id_type=MESH)

    pl.semaphore_signal(barrier, inc=1, device_id=across, device_id_type=MESH)
    peers = 1 + sum(p.astype(jnp.int32) for p in (has_up, has_down, has_right, has_left))
    pl.semaphore_wait(barrier, peers)

    def send_outer(layer, block):
        for side, sends, _ in z_sides:
            @pl.when(sends)
            def _():
                z_copy(layer, side, 0, block).start()
                z_copy(layer, side, 1, block).start()

        for side, sends, _ in j_sides:
            @pl.when(sends)
            def _():
                j_copy(layer, side, block).start()

    def send_inner(layer, block):
        for side, sends, _ in z_sides:
            @pl.when(sends)
            def _():
                z_copy(layer, side, 2, block).start()

    def send_chunk(layer, step):
        send_outer(layer, order(step))

        @pl.when(step >= LEAD)
        def _():
            send_inner(layer, order(step - LEAD))

        @pl.when(step == chunks - 1)
        def _():
            for late in range(LEAD):
                send_inner(layer, order(chunks - LEAD + late))

    @pl.loop(0, chunks)
    def _(step):
        send_chunk(0, step)

    local = pltpu.make_async_copy(x_ref, buf0.at[:, 1 : rows + 1, 1 : cols + 1], in_sem.at[0])
    small = [
        pltpu.make_async_copy(ws_hbm, ws_ref, in_sem.at[1]),
        pltpu.make_async_copy(wt_hbm, wt_ref, in_sem.at[2]),
        pltpu.make_async_copy(bias_hbm, bias_ref, in_sem.at[3]),
    ]
    for copy in small:
        copy.start()
    local.start()

    for buf in bufs:
        for row, present in ((0, has_down), (rows + 1, has_up)):
            @pl.when(jnp.logical_not(present))
            def _():
                buf[:, row] = jnp.zeros((channels, cols + 2, depth, width), BF16)

        for col, present in ((0, has_left), (cols + 1, has_right)):
            @pl.when(jnp.logical_not(present))
            def _():
                buf[:, :, col] = jnp.zeros((channels, rows + 2, depth, width), BF16)

    for copy in small:
        copy.wait()
    for layer in range(2):
        build_weights(layer, ws_ref, wt_ref, src_mat, tgt_mat)
        spare = jnp.zeros((channels, rows, cols, PAD, width), F32)
        sums[layer][:, :, :, 0:PAD] = spare
        sums[layer][:, :, :, depth + PAD : depth + 2 * PAD] = spare
        for channel in range(channels):
            sums[layer][channel, :, :, PAD : depth + PAD] = jnp.full(
                (rows, cols, depth, width), bias_ref[layer, channel], F32
            )

    lane = iota((channels * STEP, width), 1)

    def target_pass(layer, block):
        buf, total = bufs[layer], sums[layer]
        ks = rows_of(block)
        base = pl.multiple_of(block * STEP, STEP)
        for i in range(rows):
            for pair in range(cols // 2):
                shifted = [[], [], []]
                for n in range(2):
                    tile = buf[:, i + 1, 1 + 2 * pair + n, ks].reshape(channels * STEP, width)
                    wide = tile.astype(F32)
                    before = jnp.where(lane == 0, 0.0, pltpu.roll(wide, 1, 1))
                    after = jnp.where(lane == width - 1, 0.0, pltpu.roll(wide, width - 1, 1))
                    for second, piece in enumerate((before.astype(BF16), tile, after.astype(BF16))):
                        shifted[second].append(piece)
                stack = jnp.concatenate([jnp.concatenate(p, axis=1) for p in shifted], axis=0)
                got = jnp.dot(tgt_mat[layer], stack, preferred_element_type=F32)
                for n in range(2):
                    j = 2 * pair + n
                    part = got[:, width * n : width * n + width]
                    total[:, i, j, pl.ds(base + PAD, STEP)] += part[0:128].reshape(channels, STEP, width)
                    total[:, i, j, pl.ds(base + PAD + STEP, PAD)] += part[128:192].reshape(channels, PAD, width)
                    total[:, i, j, pl.ds(base, PAD)] += part[192:256].reshape(channels, PAD, width)

    def edge_start(layer):
        for half, place in ((0, depth + PAD), (1, PAD - 1)):
            @pl.when(t == half)
            def _():
                for i in range(rows):
                    for j in range(cols):
                        edge_out[layer, i, j] = sums[layer][:, i, j, place]

        e_copy(layer).start()

    def edge_add(layer):
        e_copy(layer).wait_recv()
        for half, place in ((0, depth + PAD - 1), (1, PAD)):
            @pl.when(t == half)
            def _():
                for i in range(rows):
                    for j in range(cols):
                        sums[layer][:, i, j, place] += edge_in[layer, i, j]

    def stack_of(layer, ks, pair, source_rows):
        buf = bufs[layer]
        parts = []
        for a in source_rows:
            tiles = [buf[:, a, 2 * pair + b, ks].reshape(channels * STEP, width) for b in range(4)]
            parts += [jnp.concatenate([tiles[b], tiles[b + 1]], axis=1) for b in range(3)]
        return jnp.concatenate(parts, axis=0)

    def sums_at(layer, i, j, block):
        base = pl.multiple_of(block * STEP, STEP)
        return sums[layer].at[:, i, j, pl.ds(base + PAD, STEP)]

    def own_rows_pass(layer, block):
        for pair in range(cols // 2):
            stack = stack_of(layer, rows_of(block), pair, (1, 2))
            got = jnp.dot(src_mat[layer, :, 384:1152], stack, preferred_element_type=F32)
            for i in range(rows):
                for n in range(2):
                    part = got[128 * i : 128 * i + 128, width * n : width * n + width]
                    sums_at(layer, i, 2 * pair + n, block)[...] += part.reshape(channels, STEP, width)

    def finish(layer, block):
        ks = rows_of(block)
        for pair in range(cols // 2):
            for i in range(rows):
                stack = stack_of(layer, ks, pair, (3 * i,))
                mat = src_mat[layer, 128 * i : 128 * i + 128, 1152 * i : 1152 * i + 384]
                got = jnp.dot(mat, stack, preferred_element_type=F32)
                for n in range(2):
                    j = 2 * pair + n
                    part = got[:, width * n : width * n + width].reshape(channels, STEP, width)
                    part = part + sums_at(layer, i, j, block)[...]
                    center = bufs[layer][:, i + 1, j + 1, ks].astype(F32)
                    value = (center + jnp.maximum(part, 0.0)).astype(BF16)
                    if layer == 0:
                        buf1[:, i + 1, j + 1, ks] = value
                    else:
                        staged[:, i, j, ks] = value

    def out_copy(block):
        ks = rows_of(block)
        return pltpu.make_async_copy(
            staged.at[:, :, :, ks], out_ref.at[:, :, :, ks], out_sem.at[block]
        )

    local.wait()

    @pl.loop(0, chunks)
    def _(step):
        target_pass(0, order(step))

        @pl.when(step == 0)
        def _():
            edge_start(0)

    def wait_sends():
        @pl.loop(0, chunks)
        def _(block):
            for layer in range(2):
                for side, sends, _ in z_sides:
                    @pl.when(sends)
                    def _():
                        for part in range(3):
                            z_copy(layer, side, part, block).wait_send()

                for side, sends, _ in j_sides:
                    @pl.when(sends)
                    def _():
                        j_copy(layer, side, block).wait_send()

                    for end, present in ends:
                        @pl.when(sends & present)
                        def _():
                            c_copy(layer, side, end, block).wait_send()

        for layer in range(2):
            e_copy(layer).wait_send()

    lag = LEAD + 1
    for layer in range(2):
        @pl.loop(0, chunks + lag)
        def _(step):
            @pl.when(step == lag)
            def _():
                edge_add(layer)

            if layer == 1:
                @pl.when(step == chunks + lag - 1)
                def _():
                    wait_sends()

            @pl.when(step >= lag)
            def _():
                block = order(step - lag)
                for side, _, receives in j_sides:
                    for end, present in ends:
                        @pl.when(receives & present)
                        def _():
                            c_copy(layer, side, end, block).wait_recv()

                for end, present in ends:
                    @pl.when(present)
                    def _():
                        z_copy(layer, 1 - end, 2, block).wait_recv()

                finish(layer, block)
                if layer == 0:
                    send_chunk(1, step - lag)
                    target_pass(1, block)

                    @pl.when(step == lag)
                    def _():
                        edge_start(1)
                else:
                    out_copy(block).start()

            @pl.when(step < chunks)
            def _():
                block = order(step)
                for end, present in ends:
                    @pl.when(present)
                    def _():
                        z_copy(layer, 1 - end, 0, block).wait_recv()
                        z_copy(layer, 1 - end, 1, block).wait_recv()
                        for side, sends, _ in j_sides:
                            @pl.when(sends)
                            def _():
                                c_copy(layer, side, end, block).start()

                for side, _, receives in j_sides:
                    @pl.when(receives)
                    def _():
                        j_copy(layer, side, block).wait_recv()

                own_rows_pass(layer, block)

    @pl.loop(0, chunks)
    def _(block):
        out_copy(block).wait()


def by_channels(weight):
    return jnp.transpose(weight, (0, 2, 3, 1)).reshape(-1, weight.shape[1])


def shards(sizes, volume, src_weight, tgt_weight, bias):
    channels, rows, cols, depth, width = volume.shape
    chunks = depth // STEP
    padded = pltpu.VMEM((channels, rows + 2, cols + 2, depth, width), BF16)
    total = pltpu.VMEM((channels, rows, cols, depth + 2 * PAD, width), F32)
    edges = pltpu.VMEM((2, rows, cols, channels, width), F32)
    dma = pltpu.SemaphoreType.DMA
    operands = (volume, by_channels(src_weight), by_channels(tgt_weight), bias)
    return pl.pallas_call(
        functools.partial(kernel, sizes),
        out_shape=jax.ShapeDtypeStruct(volume.shape, BF16),
        in_specs=[
            pl.BlockSpec(memory_space=pltpu.HBM),
            pl.BlockSpec(memory_space=pltpu.HBM),
            pl.BlockSpec(memory_space=pltpu.HBM),
            pl.BlockSpec(memory_space=pltpu.HBM),
        ],
        out_specs=pl.BlockSpec(memory_space=pl.ANY),
        scratch_shapes=[
            pltpu.VMEM((2 * channels * channels, 9), BF16),
            pltpu.VMEM((2 * channels * channels, 9), BF16),
            pltpu.SMEM((2, channels), F32),
            padded, padded, total, total,
            pltpu.VMEM((2, 256, 12 * 128), BF16),
            pltpu.VMEM((2, 256, 3 * 128), BF16),
            edges, edges,
            pltpu.VMEM(volume.shape, BF16),
            dma((2, 2, 3, chunks)), dma((2, 2, 3, chunks)),
            dma((2, 2, chunks)), dma((2, 2, chunks)),
            dma((2, 2, 2, chunks)), dma((2, 2, 2, chunks)),
            dma((2,)), dma((2,)),
            dma((4,)), dma((chunks,)),
        ],
        compiler_params=pltpu.CompilerParams(
            collective_id=0, has_side_effects=True, vmem_limit_bytes=40 * 1024 * 1024
        ),
    )(*(pltpu.with_memory_space_constraint(v, pltpu.HBM) for v in operands))


def solution(mesh):
    sizes = (mesh.shape["srow"], mesh.shape["scol"])
    return jax.shard_map(
        functools.partial(shards, sizes),
        mesh=mesh,
        in_specs=(P(None, "srow", "scol", "trow", None), P(), P(), P()),
        out_specs=P(None, "srow", "scol", "trow", None),
        check_vma=False,
    )
```

```python
import functools

import jax
import jax.numpy as jnp
from jax import lax
from jax.experimental import pallas as pl
from jax.experimental.pallas import tpu as pltpu
from jax.sharding import PartitionSpec as P

MESH = pl.DeviceIdType.MESH
BF16 = jnp.bfloat16
F32 = jnp.float32
STEP = 16
LEADS = (3, 3)
Z_RING = 4
PAD = 8


def iota(shape, dim):
    return lax.broadcasted_iota(jnp.int32, shape, dim)


def expand(rows, taps):
    mine = iota((64, 128), 1) // STEP == iota((64, 128), 0) % 8
    wide = [jnp.where(mine, jnp.broadcast_to(taps[:, tap : tap + 1], (64, 128)), 0.0) for tap in range(9)]
    share = rows // 8
    spread = (iota((rows, 64), 0) // share == iota((rows, 64), 1) // 8).astype(BF16)
    wide = jnp.concatenate(wide, axis=1).astype(BF16)
    return jnp.dot(spread, wide, preferred_element_type=F32)


def build_weights(layer, ws_ref, wt_ref, src_mat, tgt_mat):
    row, col = iota((128, 128), 0) % STEP, iota((128, 128), 1) % STEP
    zero = jnp.zeros((128, 128), F32)
    src = expand(128, ws_ref[pl.ds(64 * layer, 64), :].astype(F32))
    for first in range(3):
        for second in range(3):
            tap = 3 * first + second
            block = jnp.where(row == col, src[:, 128 * tap : 128 * tap + 128], zero).astype(BF16)
            for i in range(2):
                place = 128 * (3 * (first + i) + second)
                src_mat[layer, 128 * i : 128 * i + 128, place : place + 128] = block
    for second in range(3):
        for i in range(2):
            place = 128 * (3 * (3 - 3 * i) + second)
            src_mat[layer, 128 * i : 128 * i + 128, place : place + 128] = zero.astype(BF16)
    taps = wt_ref[pl.ds(64 * layer, 64), :].astype(F32)
    own = expand(128, taps)
    edge = expand(64, taps)
    edge_row, edge_col = iota((64, 128), 0) % 8, iota((64, 128), 1) % STEP
    up = (edge_row == 0) & (edge_col == STEP - 1)
    down = (edge_row == 7) & (edge_col == 0)
    for second in range(3):
        part = [slice(128 * (3 * first + second), 128 * (3 * first + second) + 128) for first in range(3)]
        block = jnp.where(col == row - 1, own[:, part[0]], zero)
        block = block + jnp.where(col == row, own[:, part[1]], zero)
        block = block + jnp.where(col == row + 1, own[:, part[2]], zero)
        place = slice(128 * second, 128 * second + 128)
        tgt_mat[layer, 0:128, place] = block.astype(BF16)
        tgt_mat[layer, 128:192, place] = jnp.where(up, edge[:, part[0]], 0.0).astype(BF16)
        tgt_mat[layer, 192:256, place] = jnp.where(down, edge[:, part[2]], 0.0).astype(BF16)


def kernel(
    sizes, x_ref, ws_hbm, wt_hbm, bias_hbm, out_ref,
    ws_ref, wt_ref, bias_ref,
    buf0, buf1, sums0, sums1, src_mat, tgt_mat, edge_out, edge_in, staged,
    z_send, z_recv, j_send, j_recv, c_send, c_recv, e_send, e_recv, in_sem, out_sem, hello,
):
    n_row, n_col = sizes
    channels, rows, cols, depth, width = x_ref.shape
    chunks = depth // STEP
    bufs, sums = (buf0, buf1), (sums0, sums1)
    r, s, t = lax.axis_index("srow"), lax.axis_index("scol"), lax.axis_index("trow")
    up, down = {"srow": lax.rem(r + 1, n_row)}, {"srow": lax.rem(r + n_row - 1, n_row)}
    right, left = {"scol": lax.rem(s + 1, n_col)}, {"scol": lax.rem(s + n_col - 1, n_col)}
    across = {"trow": 1 - t}
    has_up, has_down = r < n_row - 1, r > 0
    has_right, has_left = s < n_col - 1, s > 0

    def rows_of(block):
        return pl.ds(pl.multiple_of(block * STEP, STEP), STEP)

    def order(step):
        return (chunks - 1 - step) + t * (2 * step - (chunks - 1))

    def z_copy(layer, side, part, block):
        ks = rows_of(block)
        lo, hi = ((1, 2), (cols, cols + 1), (2, cols))[part]
        if layer == 0:
            src = x_ref.at[:, 0 if side == 0 else rows - 1, lo - 1 : hi - 1, ks]
        else:
            src = buf1.at[:, 1 if side == 0 else rows, lo:hi, ks]
        return pltpu.make_async_remote_copy(
            src_ref=src,
            dst_ref=bufs[layer].at[:, rows + 1 if side == 0 else 0, lo:hi, ks],
            send_sem=z_send.at[layer, side, part, block],
            recv_sem=z_recv.at[layer, side, part, block],
            device_id=down if side == 0 else up,
            device_id_type=MESH,
        )

    def j_copy(layer, side, block):
        ks = rows_of(block)
        if layer == 0:
            src = x_ref.at[:, :, 0 if side == 0 else cols - 1, ks]
        else:
            src = buf1.at[:, 1 : rows + 1, 1 if side == 0 else cols, ks]
        return pltpu.make_async_remote_copy(
            src_ref=src,
            dst_ref=bufs[layer].at[:, 1 : rows + 1, cols + 1 if side == 0 else 0, ks],
            send_sem=j_send.at[layer, side, block],
            recv_sem=j_recv.at[layer, side, block],
            device_id=left if side == 0 else right,
            device_id_type=MESH,
        )

    def c_copy(layer, side, end, block):
        ks = rows_of(block)
        row = 0 if end == 0 else rows + 1
        return pltpu.make_async_remote_copy(
            src_ref=bufs[layer].at[:, row, 1 if side == 0 else cols, ks],
            dst_ref=bufs[layer].at[:, row, cols + 1 if side == 0 else 0, ks],
            send_sem=c_send.at[layer, side, end, block],
            recv_sem=c_recv.at[layer, side, end, block],
            device_id=left if side == 0 else right,
            device_id_type=MESH,
        )

    def e_copy(layer):
        return pltpu.make_async_remote_copy(
            src_ref=edge_out.at[layer],
            dst_ref=edge_in.at[layer],
            send_sem=e_send.at[layer],
            recv_sem=e_recv.at[layer],
            device_id=across,
            device_id_type=MESH,
        )

    z_sides = ((0, has_down, has_up), (1, has_up, has_down))
    j_sides = ((0, has_left, has_right), (1, has_right, has_left))
    ends = ((0, has_down), (1, has_up))

    first, last = lax.rem(r, Z_RING) == 0, lax.rem(r, Z_RING) == Z_RING - 1
    up_later, down_later = has_up & jnp.logical_not(last), has_down & first
    up_earlier, down_earlier = has_up & last, has_down & jnp.logical_not(first)
    later = ((up_later, up), (down_later, down), (has_right, right), (t == 0, across))
    earlier = (
        (up_earlier, up, 1), (down_earlier, down, 0), (has_left, left, 2), (t == 1, across, 3),
    )
    barrier = pltpu.get_barrier_semaphore()
    for present, device in later:
        @pl.when(present)
        def _():
            pl.semaphore_signal(barrier, inc=1, device_id=device, device_id_type=MESH)

    awaited = sum(present.astype(jnp.int32) for present, _, _ in earlier)

    @pl.when(awaited > 0)
    def _():
        pl.semaphore_wait(barrier, awaited)

    for present, device, slot in earlier:
        @pl.when(present)
        def _():
            pl.semaphore_signal(hello.at[slot], inc=1, device_id=device, device_id_type=MESH)

    def send_rows(layer, side, step):
        z_copy(layer, side, 0, order(step)).start()
        z_copy(layer, side, 1, order(step)).start()

        lead = LEADS[layer]

        @pl.when(step >= lead)
        def _():
            z_copy(layer, side, 2, order(step - lead)).start()

        @pl.when(step == chunks - 1)
        def _():
            for late in range(lead):
                z_copy(layer, side, 2, order(chunks - lead + late)).start()

    def send_cols(layer, side, step):
        j_copy(layer, side, order(step)).start()

    def send_chunk(layer, step):
        for side, sends, _ in z_sides:
            @pl.when(sends)
            def _():
                send_rows(layer, side, step)

        for side, sends, _ in j_sides:
            @pl.when(sends)
            def _():
                send_cols(layer, side, step)

    def send_first(send, side, present, slot=None):
        @pl.when(present)
        def _():
            if slot is not None:
                pl.semaphore_wait(hello.at[slot], 1)

            @pl.loop(0, chunks)
            def _(step):
                send(0, side, step)

    send_first(send_rows, 0, down_earlier)
    send_first(send_rows, 1, up_earlier)
    send_first(send_cols, 0, has_left)

    local = pltpu.make_async_copy(x_ref, buf0.at[:, 1 : rows + 1, 1 : cols + 1], in_sem.at[0])
    small = [
        pltpu.make_async_copy(ws_hbm, ws_ref, in_sem.at[1]),
        pltpu.make_async_copy(wt_hbm, wt_ref, in_sem.at[2]),
        pltpu.make_async_copy(bias_hbm, bias_ref, in_sem.at[3]),
    ]
    for copy in small:
        copy.start()
    local.start()
    send_first(send_rows, 1, up_later, 0)
    send_first(send_cols, 1, has_right, 2)
    send_first(send_rows, 0, down_later, 1)

    @pl.when(t == 0)
    def _():
        pl.semaphore_wait(hello.at[3], 1)

    for buf in bufs:
        for row, present in ((0, has_down), (rows + 1, has_up)):
            @pl.when(jnp.logical_not(present))
            def _():
                buf[:, row] = jnp.zeros((channels, cols + 2, depth, width), BF16)

        for col, present in ((0, has_left), (cols + 1, has_right)):
            @pl.when(jnp.logical_not(present))
            def _():
                buf[:, :, col] = jnp.zeros((channels, rows + 2, depth, width), BF16)

    for copy in small:
        copy.wait()
    for layer in range(2):
        build_weights(layer, ws_ref, wt_ref, src_mat, tgt_mat)
        spare = jnp.zeros((channels, rows, cols, PAD, width), F32)
        sums[layer][:, :, :, 0:PAD] = spare
        sums[layer][:, :, :, depth + PAD : depth + 2 * PAD] = spare
        for channel in range(channels):
            sums[layer][channel, :, :, PAD : depth + PAD] = jnp.full(
                (rows, cols, depth, width), bias_ref[layer, channel], F32
            )

    lane = iota((channels * STEP, width), 1)

    def target_pass(layer, block):
        buf, total = bufs[layer], sums[layer]
        ks = rows_of(block)
        base = pl.multiple_of(block * STEP, STEP)
        for i in range(rows):
            for pair in range(cols // 2):
                shifted = [[], [], []]
                for n in range(2):
                    tile = buf[:, i + 1, 1 + 2 * pair + n, ks].reshape(channels * STEP, width)
                    wide = tile.astype(F32)
                    before = jnp.where(lane == 0, 0.0, pltpu.roll(wide, 1, 1))
                    after = jnp.where(lane == width - 1, 0.0, pltpu.roll(wide, width - 1, 1))
                    for second, piece in enumerate((before.astype(BF16), tile, after.astype(BF16))):
                        shifted[second].append(piece)
                stack = jnp.concatenate([jnp.concatenate(p, axis=1) for p in shifted], axis=0)
                got = jnp.dot(tgt_mat[layer], stack, preferred_element_type=F32)
                for n in range(2):
                    j = 2 * pair + n
                    part = got[:, width * n : width * n + width]
                    total[:, i, j, pl.ds(base + PAD, STEP)] += part[0:128].reshape(channels, STEP, width)
                    total[:, i, j, pl.ds(base + PAD + STEP, PAD)] += part[128:192].reshape(channels, PAD, width)
                    total[:, i, j, pl.ds(base, PAD)] += part[192:256].reshape(channels, PAD, width)

    def edge_start(layer):
        for half, place in ((0, depth + PAD), (1, PAD - 1)):
            @pl.when(t == half)
            def _():
                for i in range(rows):
                    for j in range(cols):
                        edge_out[layer, i, j] = sums[layer][:, i, j, place]

        e_copy(layer).start()

    def edge_add(layer):
        e_copy(layer).wait_recv()
        for half, place in ((0, depth + PAD - 1), (1, PAD)):
            @pl.when(t == half)
            def _():
                for i in range(rows):
                    for j in range(cols):
                        sums[layer][:, i, j, place] += edge_in[layer, i, j]

    def stack_of(layer, ks, pair, source_rows):
        buf = bufs[layer]
        parts = []
        for a in source_rows:
            tiles = [buf[:, a, 2 * pair + b, ks].reshape(channels * STEP, width) for b in range(4)]
            parts += [jnp.concatenate([tiles[b], tiles[b + 1]], axis=1) for b in range(3)]
        return jnp.concatenate(parts, axis=0)

    def sums_at(layer, i, j, block):
        base = pl.multiple_of(block * STEP, STEP)
        return sums[layer].at[:, i, j, pl.ds(base + PAD, STEP)]

    def own_rows_pass(layer, block):
        for pair in range(cols // 2):
            stack = stack_of(layer, rows_of(block), pair, (1, 2))
            got = jnp.dot(src_mat[layer, :, 384:1152], stack, preferred_element_type=F32)
            for i in range(rows):
                for n in range(2):
                    part = got[128 * i : 128 * i + 128, width * n : width * n + width]
                    sums_at(layer, i, 2 * pair + n, block)[...] += part.reshape(channels, STEP, width)

    def finish(layer, block):
        ks = rows_of(block)
        for pair in range(cols // 2):
            for i in range(rows):
                stack = stack_of(layer, ks, pair, (3 * i,))
                mat = src_mat[layer, 128 * i : 128 * i + 128, 1152 * i : 1152 * i + 384]
                got = jnp.dot(mat, stack, preferred_element_type=F32)
                for n in range(2):
                    j = 2 * pair + n
                    part = got[:, width * n : width * n + width].reshape(channels, STEP, width)
                    part = part + sums_at(layer, i, j, block)[...]
                    center = bufs[layer][:, i + 1, j + 1, ks].astype(F32)
                    value = (center + jnp.maximum(part, 0.0)).astype(BF16)
                    if layer == 0:
                        buf1[:, i + 1, j + 1, ks] = value
                    else:
                        staged[:, i, j, ks] = value

    def out_copy(block):
        ks = rows_of(block)
        return pltpu.make_async_copy(
            staged.at[:, :, :, ks], out_ref.at[:, :, :, ks], out_sem.at[block]
        )

    local.wait()

    @pl.loop(0, chunks)
    def _(step):
        target_pass(0, order(step))

        @pl.when(step == 0)
        def _():
            edge_start(0)

    def wait_sends():
        @pl.loop(0, chunks)
        def _(block):
            for layer in range(2):
                for side, sends, _ in z_sides:
                    @pl.when(sends)
                    def _():
                        for part in range(3):
                            z_copy(layer, side, part, block).wait_send()

                for side, sends, _ in j_sides:
                    @pl.when(sends)
                    def _():
                        j_copy(layer, side, block).wait_send()

                    for end, present in ends:
                        @pl.when(sends & present)
                        def _():
                            c_copy(layer, side, end, block).wait_send()

        for layer in range(2):
            e_copy(layer).wait_send()

    for layer in range(2):
        lag = LEADS[layer] + 1

        @pl.loop(0, chunks + lag)
        def _(step):
            @pl.when(step == lag)
            def _():
                edge_add(layer)

            if layer == 1:
                @pl.when(step == chunks + lag - 1)
                def _():
                    wait_sends()

            @pl.when(step >= lag)
            def _():
                block = order(step - lag)
                for side, _, receives in j_sides:
                    for end, present in ends:
                        @pl.when(receives & present)
                        def _():
                            c_copy(layer, side, end, block).wait_recv()

                for end, present in ends:
                    @pl.when(present)
                    def _():
                        z_copy(layer, 1 - end, 2, block).wait_recv()

                finish(layer, block)
                if layer == 0:
                    send_chunk(1, step - lag)
                    target_pass(1, block)

                    @pl.when(step == lag)
                    def _():
                        edge_start(1)
                else:
                    out_copy(block).start()

            @pl.when(step < chunks)
            def _():
                block = order(step)
                for end, present in ends:
                    @pl.when(present)
                    def _():
                        z_copy(layer, 1 - end, 0, block).wait_recv()
                        z_copy(layer, 1 - end, 1, block).wait_recv()
                        for side, sends, _ in j_sides:
                            @pl.when(sends)
                            def _():
                                c_copy(layer, side, end, block).start()

                for side, _, receives in j_sides:
                    @pl.when(receives)
                    def _():
                        j_copy(layer, side, block).wait_recv()

                own_rows_pass(layer, block)

    @pl.loop(0, chunks)
    def _(block):
        out_copy(block).wait()


def by_channels(weight):
    return jnp.transpose(weight, (0, 2, 3, 1)).reshape(-1, weight.shape[1])


def shards(sizes, volume, src_weight, tgt_weight, bias):
    channels, rows, cols, depth, width = volume.shape
    chunks = depth // STEP
    padded = pltpu.VMEM((channels, rows + 2, cols + 2, depth, width), BF16)
    total = pltpu.VMEM((channels, rows, cols, depth + 2 * PAD, width), F32)
    edges = pltpu.VMEM((2, rows, cols, channels, width), F32)
    dma = pltpu.SemaphoreType.DMA
    operands = (volume, by_channels(src_weight), by_channels(tgt_weight), bias)
    return pl.pallas_call(
        functools.partial(kernel, sizes),
        out_shape=jax.ShapeDtypeStruct(volume.shape, BF16),
        in_specs=[
            pl.BlockSpec(memory_space=pltpu.HBM),
            pl.BlockSpec(memory_space=pltpu.HBM),
            pl.BlockSpec(memory_space=pltpu.HBM),
            pl.BlockSpec(memory_space=pltpu.HBM),
        ],
        out_specs=pl.BlockSpec(memory_space=pl.ANY),
        scratch_shapes=[
            pltpu.VMEM((2 * channels * channels, 9), BF16),
            pltpu.VMEM((2 * channels * channels, 9), BF16),
            pltpu.SMEM((2, channels), F32),
            padded, padded, total, total,
            pltpu.VMEM((2, 256, 12 * 128), BF16),
            pltpu.VMEM((2, 256, 3 * 128), BF16),
            edges, edges,
            pltpu.VMEM(volume.shape, BF16),
            dma((2, 2, 3, chunks)), dma((2, 2, 3, chunks)),
            dma((2, 2, chunks)), dma((2, 2, chunks)),
            dma((2, 2, 2, chunks)), dma((2, 2, 2, chunks)),
            dma((2,)), dma((2,)),
            dma((4,)), dma((chunks,)),
            pltpu.SemaphoreType.REGULAR((4,)),
        ],
        compiler_params=pltpu.CompilerParams(
            collective_id=0, has_side_effects=True, vmem_limit_bytes=40 * 1024 * 1024
        ),
    )(*(pltpu.with_memory_space_constraint(v, pltpu.HBM) for v in operands))


def solution(mesh):
    sizes = (mesh.shape["srow"], mesh.shape["scol"])
    return jax.shard_map(
        functools.partial(shards, sizes),
        mesh=mesh,
        in_specs=(P(None, "srow", "scol", "trow", None), P(), P(), P()),
        out_specs=P(None, "srow", "scol", "trow", None),
        check_vma=False,
    )
```

```python
import functools

import jax
import jax.numpy as jnp
from jax import lax
from jax.experimental import pallas as pl
from jax.experimental.pallas import tpu as pltpu
from jax.sharding import PartitionSpec as P

MESH = pl.DeviceIdType.MESH
BF16 = jnp.bfloat16
F32 = jnp.float32
STEP = 16
FAR, NEAR, INNER = 0, 1, 2
ORDERS = (
    ((FAR, 0), (NEAR, 0), (FAR, 1), (NEAR, 1), (FAR, 2), (NEAR, 2), (FAR, 3), (NEAR, 3), (INNER, 0), (INNER, 1), (INNER, 2), (INNER, 3)),
    ((FAR, 0), (NEAR, 0), (FAR, 1), (NEAR, 1), (FAR, 2), (NEAR, 2), (FAR, 3), (NEAR, 3), (INNER, 0), (INNER, 1), (INNER, 2), (INNER, 3)),
)
Z_RING = 4
PAD = 8


def iota(shape, dim):
    return lax.broadcasted_iota(jnp.int32, shape, dim)


def expand(rows, taps):
    mine = iota((64, 128), 1) // STEP == iota((64, 128), 0) % 8
    wide = [jnp.where(mine, jnp.broadcast_to(taps[:, tap : tap + 1], (64, 128)), 0.0) for tap in range(9)]
    share = rows // 8
    spread = (iota((rows, 64), 0) // share == iota((rows, 64), 1) // 8).astype(BF16)
    wide = jnp.concatenate(wide, axis=1).astype(BF16)
    return jnp.dot(spread, wide, preferred_element_type=F32)


def build_weights(layer, ws_ref, wt_ref, src_mat, tgt_mat):
    row, col = iota((128, 128), 0) % STEP, iota((128, 128), 1) % STEP
    zero = jnp.zeros((128, 128), F32)
    src = expand(128, ws_ref[pl.ds(64 * layer, 64), :].astype(F32))
    for first in range(3):
        for second in range(3):
            tap = 3 * first + second
            block = jnp.where(row == col, src[:, 128 * tap : 128 * tap + 128], zero).astype(BF16)
            for i in range(2):
                place = 128 * (3 * (first + i) + second)
                src_mat[layer, 128 * i : 128 * i + 128, place : place + 128] = block
    for second in range(3):
        for i in range(2):
            place = 128 * (3 * (3 - 3 * i) + second)
            src_mat[layer, 128 * i : 128 * i + 128, place : place + 128] = zero.astype(BF16)
    taps = wt_ref[pl.ds(64 * layer, 64), :].astype(F32)
    own = expand(128, taps)
    edge = expand(64, taps)
    edge_row, edge_col = iota((64, 128), 0) % 8, iota((64, 128), 1) % STEP
    up = (edge_row == 0) & (edge_col == STEP - 1)
    down = (edge_row == 7) & (edge_col == 0)
    for second in range(3):
        part = [slice(128 * (3 * first + second), 128 * (3 * first + second) + 128) for first in range(3)]
        block = jnp.where(col == row - 1, own[:, part[0]], zero)
        block = block + jnp.where(col == row, own[:, part[1]], zero)
        block = block + jnp.where(col == row + 1, own[:, part[2]], zero)
        place = slice(128 * second, 128 * second + 128)
        tgt_mat[layer, 0:128, place] = block.astype(BF16)
        tgt_mat[layer, 128:192, place] = jnp.where(up, edge[:, part[0]], 0.0).astype(BF16)
        tgt_mat[layer, 192:256, place] = jnp.where(down, edge[:, part[2]], 0.0).astype(BF16)


def kernel(
    sizes, x_ref, ws_hbm, wt_hbm, bias_hbm, out_ref,
    ws_ref, wt_ref, bias_ref,
    buf0, buf1, sums0, sums1, src_mat, tgt_mat, edge_out, edge_in, staged,
    z_send, z_recv, j_send, j_recv, c_send, c_recv, e_send, e_recv, in_sem, out_sem, hello,
):
    n_row, n_col = sizes
    channels, rows, cols, depth, width = x_ref.shape
    chunks = depth // STEP
    bufs, sums = (buf0, buf1), (sums0, sums1)
    r, s, t = lax.axis_index("srow"), lax.axis_index("scol"), lax.axis_index("trow")
    up, down = {"srow": lax.rem(r + 1, n_row)}, {"srow": lax.rem(r + n_row - 1, n_row)}
    right, left = {"scol": lax.rem(s + 1, n_col)}, {"scol": lax.rem(s + n_col - 1, n_col)}
    across = {"trow": 1 - t}
    has_up, has_down = r < n_row - 1, r > 0
    has_right, has_left = s < n_col - 1, s > 0

    def rows_of(block):
        return pl.ds(pl.multiple_of(block * STEP, STEP), STEP)

    def order(step):
        return (chunks - 1 - step) + t * (2 * step - (chunks - 1))

    odd = lax.rem(s, 2)
    part_cols = (
        pl.ds(1 + (cols - 1) * odd, 1), pl.ds(cols - (cols - 1) * odd, 1), pl.ds(2, cols - 2),
    )
    part_cols_in = (
        pl.ds((cols - 1) * odd, 1), pl.ds(cols - 1 - (cols - 1) * odd, 1), pl.ds(1, cols - 2),
    )

    def z_copy(layer, side, part, block):
        ks = rows_of(block)
        if layer == 0:
            src = x_ref.at[:, 0 if side == 0 else rows - 1, part_cols_in[part], ks]
        else:
            src = buf1.at[:, 1 if side == 0 else rows, part_cols[part], ks]
        return pltpu.make_async_remote_copy(
            src_ref=src,
            dst_ref=bufs[layer].at[:, rows + 1 if side == 0 else 0, part_cols[part], ks],
            send_sem=z_send.at[layer, side, part, block],
            recv_sem=z_recv.at[layer, side, part, block],
            device_id=down if side == 0 else up,
            device_id_type=MESH,
        )

    def j_copy(layer, side, block):
        ks = rows_of(block)
        if layer == 0:
            src = x_ref.at[:, :, 0 if side == 0 else cols - 1, ks]
        else:
            src = buf1.at[:, 1 : rows + 1, 1 if side == 0 else cols, ks]
        return pltpu.make_async_remote_copy(
            src_ref=src,
            dst_ref=bufs[layer].at[:, 1 : rows + 1, cols + 1 if side == 0 else 0, ks],
            send_sem=j_send.at[layer, side, block],
            recv_sem=j_recv.at[layer, side, block],
            device_id=left if side == 0 else right,
            device_id_type=MESH,
        )

    far_side = {"scol": lax.rem(s + n_col - 1 + 2 * odd, n_col)}
    near_side = {"scol": lax.rem(s + n_col + 1 - 2 * odd, n_col)}

    def c_copy(layer, part, end, block):
        ks = rows_of(block)
        row = 0 if end == 0 else rows + 1
        to_right = odd if part == FAR else 1 - odd
        return pltpu.make_async_remote_copy(
            src_ref=bufs[layer].at[:, row, 1 + (cols - 1) * to_right, ks],
            dst_ref=bufs[layer].at[:, row, (cols + 1) * (1 - to_right), ks],
            send_sem=c_send.at[layer, part, end, block],
            recv_sem=c_recv.at[layer, part, end, block],
            device_id=far_side if part == FAR else near_side,
            device_id_type=MESH,
        )

    def e_copy(layer):
        return pltpu.make_async_remote_copy(
            src_ref=edge_out.at[layer],
            dst_ref=edge_in.at[layer],
            send_sem=e_send.at[layer],
            recv_sem=e_recv.at[layer],
            device_id=across,
            device_id_type=MESH,
        )

    z_sides = ((0, has_down, has_up), (1, has_up, has_down))
    j_sides = ((0, has_left, has_right), (1, has_right, has_left))
    ends = ((0, has_down), (1, has_up))
    has_far = (has_right & (odd == 1)) | (has_left & (odd == 0))
    has_near = (has_right & (odd == 0)) | (has_left & (odd == 1))
    beside = (has_far, has_near)

    first, last = lax.rem(r, Z_RING) == 0, lax.rem(r, Z_RING) == Z_RING - 1
    up_later, down_later = has_up & jnp.logical_not(last), has_down & first
    up_earlier, down_earlier = has_up & last, has_down & jnp.logical_not(first)
    later = ((up_later, up), (down_later, down), (has_right, right), (t == 0, across))
    earlier = (
        (up_earlier, up, 1), (down_earlier, down, 0), (has_left, left, 2), (t == 1, across, 3),
    )
    barrier = pltpu.get_barrier_semaphore()
    for present, device in later:
        @pl.when(present)
        def _():
            pl.semaphore_signal(barrier, inc=1, device_id=device, device_id_type=MESH)

    awaited = sum(present.astype(jnp.int32) for present, _, _ in earlier)

    @pl.when(awaited > 0)
    def _():
        pl.semaphore_wait(barrier, awaited)

    for present, device, slot in earlier:
        @pl.when(present)
        def _():
            pl.semaphore_signal(hello.at[slot], inc=1, device_id=device, device_id_type=MESH)

    def send_rows(layer, side, items):
        for part, step in items:
            z_copy(layer, side, part, order(step)).start()

    def send_cols(layer, side, items):
        for part, step in items:
            if part == FAR:
                j_copy(layer, side, order(step)).start()

    def send_items(layer, items):
        for side, sends, _ in z_sides:
            @pl.when(sends)
            def _():
                send_rows(layer, side, items)

        for side, sends, _ in j_sides:
            @pl.when(sends)
            def _():
                send_cols(layer, side, items)

    def send_first(send, side, present, slot=None):
        @pl.when(present)
        def _():
            if slot is not None:
                pl.semaphore_wait(hello.at[slot], 1)
            send(0, side, ORDERS[0])

    send_first(send_rows, 0, down_earlier)
    send_first(send_rows, 1, up_earlier)
    send_first(send_cols, 0, has_left)

    local = pltpu.make_async_copy(x_ref, buf0.at[:, 1 : rows + 1, 1 : cols + 1], in_sem.at[0])
    small = [
        pltpu.make_async_copy(ws_hbm, ws_ref, in_sem.at[1]),
        pltpu.make_async_copy(wt_hbm, wt_ref, in_sem.at[2]),
        pltpu.make_async_copy(bias_hbm, bias_ref, in_sem.at[3]),
    ]
    for copy in small:
        copy.start()
    local.start()
    send_first(send_rows, 1, up_later, 0)
    send_first(send_cols, 1, has_right, 2)
    send_first(send_rows, 0, down_later, 1)

    @pl.when(t == 0)
    def _():
        pl.semaphore_wait(hello.at[3], 1)

    for buf in bufs:
        for row, present in ((0, has_down), (rows + 1, has_up)):
            @pl.when(jnp.logical_not(present))
            def _():
                buf[:, row] = jnp.zeros((channels, cols + 2, depth, width), BF16)

        for col, present in ((0, has_left), (cols + 1, has_right)):
            @pl.when(jnp.logical_not(present))
            def _():
                buf[:, :, col] = jnp.zeros((channels, rows + 2, depth, width), BF16)

    for copy in small:
        copy.wait()
    for layer in range(2):
        build_weights(layer, ws_ref, wt_ref, src_mat, tgt_mat)
        spare = jnp.zeros((channels, rows, cols, PAD, width), F32)
        sums[layer][:, :, :, 0:PAD] = spare
        sums[layer][:, :, :, depth + PAD : depth + 2 * PAD] = spare
        for channel in range(channels):
            sums[layer][channel, :, :, PAD : depth + PAD] = jnp.full(
                (rows, cols, depth, width), bias_ref[layer, channel], F32
            )

    lane = iota((channels * STEP, width), 1)

    def target_pass(layer, block):
        buf, total = bufs[layer], sums[layer]
        ks = rows_of(block)
        base = pl.multiple_of(block * STEP, STEP)
        for i in range(rows):
            for pair in range(cols // 2):
                shifted = [[], [], []]
                for n in range(2):
                    tile = buf[:, i + 1, 1 + 2 * pair + n, ks].reshape(channels * STEP, width)
                    wide = tile.astype(F32)
                    before = jnp.where(lane == 0, 0.0, pltpu.roll(wide, 1, 1))
                    after = jnp.where(lane == width - 1, 0.0, pltpu.roll(wide, width - 1, 1))
                    for second, piece in enumerate((before.astype(BF16), tile, after.astype(BF16))):
                        shifted[second].append(piece)
                stack = jnp.concatenate([jnp.concatenate(p, axis=1) for p in shifted], axis=0)
                got = jnp.dot(tgt_mat[layer], stack, preferred_element_type=F32)
                for n in range(2):
                    j = 2 * pair + n
                    part = got[:, width * n : width * n + width]
                    total[:, i, j, pl.ds(base + PAD, STEP)] += part[0:128].reshape(channels, STEP, width)
                    total[:, i, j, pl.ds(base + PAD + STEP, PAD)] += part[128:192].reshape(channels, PAD, width)
                    total[:, i, j, pl.ds(base, PAD)] += part[192:256].reshape(channels, PAD, width)

    def edge_start(layer):
        for half, place in ((0, depth + PAD), (1, PAD - 1)):
            @pl.when(t == half)
            def _():
                for i in range(rows):
                    for j in range(cols):
                        edge_out[layer, i, j] = sums[layer][:, i, j, place]

        e_copy(layer).start()

    def edge_add(layer):
        e_copy(layer).wait_recv()
        for half, place in ((0, depth + PAD - 1), (1, PAD)):
            @pl.when(t == half)
            def _():
                for i in range(rows):
                    for j in range(cols):
                        sums[layer][:, i, j, place] += edge_in[layer, i, j]

    def stack_of(layer, ks, pair, source_rows):
        buf = bufs[layer]
        parts = []
        for a in source_rows:
            tiles = [buf[:, a, 2 * pair + b, ks].reshape(channels * STEP, width) for b in range(4)]
            parts += [jnp.concatenate([tiles[b], tiles[b + 1]], axis=1) for b in range(3)]
        return jnp.concatenate(parts, axis=0)

    def sums_at(layer, i, j, block):
        base = pl.multiple_of(block * STEP, STEP)
        return sums[layer].at[:, i, j, pl.ds(base + PAD, STEP)]

    def own_rows_pass(layer, block):
        for pair in range(cols // 2):
            stack = stack_of(layer, rows_of(block), pair, (1, 2))
            got = jnp.dot(src_mat[layer, :, 384:1152], stack, preferred_element_type=F32)
            for i in range(rows):
                for n in range(2):
                    part = got[128 * i : 128 * i + 128, width * n : width * n + width]
                    sums_at(layer, i, 2 * pair + n, block)[...] += part.reshape(channels, STEP, width)

    def finish(layer, block):
        ks = rows_of(block)
        for pair in range(cols // 2):
            for i in range(rows):
                stack = stack_of(layer, ks, pair, (3 * i,))
                mat = src_mat[layer, 128 * i : 128 * i + 128, 1152 * i : 1152 * i + 384]
                got = jnp.dot(mat, stack, preferred_element_type=F32)
                for n in range(2):
                    j = 2 * pair + n
                    part = got[:, width * n : width * n + width].reshape(channels, STEP, width)
                    part = part + sums_at(layer, i, j, block)[...]
                    center = bufs[layer][:, i + 1, j + 1, ks].astype(F32)
                    value = (center + jnp.maximum(part, 0.0)).astype(BF16)
                    if layer == 0:
                        buf1[:, i + 1, j + 1, ks] = value
                    else:
                        staged[:, i, j, ks] = value

    def out_copy(block):
        ks = rows_of(block)
        return pltpu.make_async_copy(
            staged.at[:, :, :, ks], out_ref.at[:, :, :, ks], out_sem.at[block]
        )

    local.wait()

    @pl.loop(0, chunks)
    def _(step):
        target_pass(0, order(step))

        @pl.when(step == 0)
        def _():
            edge_start(0)

    def wait_sends():
        @pl.loop(0, chunks)
        def _(block):
            for layer in range(2):
                for side, sends, _ in z_sides:
                    @pl.when(sends)
                    def _():
                        for part in range(3):
                            z_copy(layer, side, part, block).wait_send()

                for side, sends, _ in j_sides:
                    @pl.when(sends)
                    def _():
                        j_copy(layer, side, block).wait_send()

                for part in (FAR, NEAR):
                    for end, present in ends:
                        @pl.when(beside[part] & present)
                        def _():
                            c_copy(layer, part, end, block).wait_send()

        for layer in range(2):
            e_copy(layer).wait_send()

    def take_outer(layer, part, step):
        block = order(step)
        for end, present in ends:
            @pl.when(present)
            def _():
                z_copy(layer, 1 - end, part, block).wait_recv()

                @pl.when(beside[part])
                def _():
                    c_copy(layer, part, end, block).start()

    def take_cols(layer, step):
        block = order(step)
        for side, _, receives in j_sides:
            @pl.when(receives)
            def _():
                j_copy(layer, side, block).wait_recv()

        own_rows_pass(layer, block)

    def take_inner(layer, step):
        block = order(step)
        for part in (FAR, NEAR):
            for end, present in ends:
                @pl.when(beside[part] & present)
                def _():
                    c_copy(layer, part, end, block).wait_recv()

        for end, present in ends:
            @pl.when(present)
            def _():
                z_copy(layer, 1 - end, INNER, block).wait_recv()

        finish(layer, block)

    unsent = list(ORDERS[1])
    for layer in range(2):
        for part, step in ORDERS[layer]:
            if part != INNER:
                take_outer(layer, part, step)
                if part == NEAR:
                    take_cols(layer, step)
                continue
            if step == 0:
                edge_add(layer)
            if layer == 1 and step == chunks - 1:
                wait_sends()
            take_inner(layer, step)
            if layer == 1:
                out_copy(order(step)).start()
                continue
            ready = []
            while unsent and unsent[0][1] <= step:
                ready.append(unsent.pop(0))
            send_items(1, ready)
            target_pass(1, order(step))
            if step == 0:
                edge_start(1)

    @pl.loop(0, chunks)
    def _(block):
        out_copy(block).wait()


def by_channels(weight):
    return jnp.transpose(weight, (0, 2, 3, 1)).reshape(-1, weight.shape[1])


def shards(sizes, volume, src_weight, tgt_weight, bias):
    channels, rows, cols, depth, width = volume.shape
    chunks = depth // STEP
    padded = pltpu.VMEM((channels, rows + 2, cols + 2, depth, width), BF16)
    total = pltpu.VMEM((channels, rows, cols, depth + 2 * PAD, width), F32)
    edges = pltpu.VMEM((2, rows, cols, channels, width), F32)
    dma = pltpu.SemaphoreType.DMA
    operands = (volume, by_channels(src_weight), by_channels(tgt_weight), bias)
    return pl.pallas_call(
        functools.partial(kernel, sizes),
        out_shape=jax.ShapeDtypeStruct(volume.shape, BF16),
        in_specs=[
            pl.BlockSpec(memory_space=pltpu.HBM),
            pl.BlockSpec(memory_space=pltpu.HBM),
            pl.BlockSpec(memory_space=pltpu.HBM),
            pl.BlockSpec(memory_space=pltpu.HBM),
        ],
        out_specs=pl.BlockSpec(memory_space=pl.ANY),
        scratch_shapes=[
            pltpu.VMEM((2 * channels * channels, 9), BF16),
            pltpu.VMEM((2 * channels * channels, 9), BF16),
            pltpu.SMEM((2, channels), F32),
            padded, padded, total, total,
            pltpu.VMEM((2, 256, 12 * 128), BF16),
            pltpu.VMEM((2, 256, 3 * 128), BF16),
            edges, edges,
            pltpu.VMEM(volume.shape, BF16),
            dma((2, 2, 3, chunks)), dma((2, 2, 3, chunks)),
            dma((2, 2, chunks)), dma((2, 2, chunks)),
            dma((2, 2, 2, chunks)), dma((2, 2, 2, chunks)),
            dma((2,)), dma((2,)),
            dma((4,)), dma((chunks,)),
            pltpu.SemaphoreType.REGULAR((4,)),
        ],
        compiler_params=pltpu.CompilerParams(
            collective_id=0, has_side_effects=True, vmem_limit_bytes=40 * 1024 * 1024
        ),
    )(*(pltpu.with_memory_space_constraint(v, pltpu.HBM) for v in operands))


def solution(mesh):
    sizes = (mesh.shape["srow"], mesh.shape["scol"])
    return jax.shard_map(
        functools.partial(shards, sizes),
        mesh=mesh,
        in_specs=(P(None, "srow", "scol", "trow", None), P(), P(), P()),
        out_specs=P(None, "srow", "scol", "trow", None),
        check_vma=False,
    )
```

```python
import functools

import jax
import jax.numpy as jnp
from jax import lax
from jax.experimental import pallas as pl
from jax.experimental.pallas import tpu as pltpu
from jax.sharding import PartitionSpec as P

MESH = pl.DeviceIdType.MESH
BF16 = jnp.bfloat16
F32 = jnp.float32
STEP = 16
FAR, NEAR, INNER = 0, 1, 2
ORDERS = (
    ((FAR, 0), (NEAR, 0), (FAR, 1), (NEAR, 1), (FAR, 2), (NEAR, 2), (FAR, 3), (NEAR, 3), (INNER, 0), (INNER, 1), (INNER, 2), (INNER, 3)),
    ((FAR, 0), (NEAR, 0), (FAR, 1), (NEAR, 1), (FAR, 2), (NEAR, 2), (FAR, 3), (NEAR, 3), (INNER, 0), (INNER, 1), (INNER, 2), (INNER, 3)),
)
Z_RING = 4
PAD = 8


def iota(shape, dim):
    return lax.broadcasted_iota(jnp.int32, shape, dim)


def expand(rows, taps):
    mine = iota((64, 128), 1) // STEP == iota((64, 128), 0) % 8
    wide = [jnp.where(mine, jnp.broadcast_to(taps[:, tap : tap + 1], (64, 128)), 0.0) for tap in range(9)]
    share = rows // 8
    spread = (iota((rows, 64), 0) // share == iota((rows, 64), 1) // 8).astype(BF16)
    wide = jnp.concatenate(wide, axis=1).astype(BF16)
    return jnp.dot(spread, wide, preferred_element_type=F32)


def build_weights(layer, ws_ref, wt_ref, src_mat, tgt_mat):
    row, col = iota((128, 128), 0) % STEP, iota((128, 128), 1) % STEP
    zero = jnp.zeros((128, 128), F32)
    src = expand(128, ws_ref[pl.ds(64 * layer, 64), :].astype(F32))
    for first in range(3):
        for second in range(3):
            tap = 3 * first + second
            block = jnp.where(row == col, src[:, 128 * tap : 128 * tap + 128], zero).astype(BF16)
            for i in range(2):
                place = 128 * (3 * (first + i) + second)
                src_mat[layer, 128 * i : 128 * i + 128, place : place + 128] = block
    for second in range(3):
        for i in range(2):
            place = 128 * (3 * (3 - 3 * i) + second)
            src_mat[layer, 128 * i : 128 * i + 128, place : place + 128] = zero.astype(BF16)
    taps = wt_ref[pl.ds(64 * layer, 64), :].astype(F32)
    own = expand(128, taps)
    edge = expand(64, taps)
    edge_row, edge_col = iota((64, 128), 0) % 8, iota((64, 128), 1) % STEP
    up = (edge_row == 0) & (edge_col == STEP - 1)
    down = (edge_row == 7) & (edge_col == 0)
    for second in range(3):
        part = [slice(128 * (3 * first + second), 128 * (3 * first + second) + 128) for first in range(3)]
        block = jnp.where(col == row - 1, own[:, part[0]], zero)
        block = block + jnp.where(col == row, own[:, part[1]], zero)
        block = block + jnp.where(col == row + 1, own[:, part[2]], zero)
        place = slice(128 * second, 128 * second + 128)
        tgt_mat[layer, 0:128, place] = block.astype(BF16)
        tgt_mat[layer, 128:192, place] = jnp.where(up, edge[:, part[0]], 0.0).astype(BF16)
        tgt_mat[layer, 192:256, place] = jnp.where(down, edge[:, part[2]], 0.0).astype(BF16)


def kernel(
    sizes, x_ref, ws_hbm, wt_hbm, bias_hbm, out_ref,
    ws_ref, wt_ref, bias_ref,
    buf0, buf1, sums0, sums1, src_mat, tgt_mat, edge_out, edge_in,
    z_send, z_recv, j_send, j_recv, c_send, c_recv, e_send, e_recv, in_sem, hello,
):
    n_row, n_col = sizes
    channels, rows, cols, depth, width = x_ref.shape
    chunks = depth // STEP
    bufs, sums = (buf0, buf1), (sums0, sums1)
    r, s, t = lax.axis_index("srow"), lax.axis_index("scol"), lax.axis_index("trow")
    up, down = {"srow": lax.rem(r + 1, n_row)}, {"srow": lax.rem(r + n_row - 1, n_row)}
    right, left = {"scol": lax.rem(s + 1, n_col)}, {"scol": lax.rem(s + n_col - 1, n_col)}
    across = {"trow": 1 - t}
    has_up, has_down = r < n_row - 1, r > 0
    has_right, has_left = s < n_col - 1, s > 0

    def rows_of(block):
        return pl.ds(pl.multiple_of(block * STEP, STEP), STEP)

    def order(step):
        return (chunks - 1 - step) + t * (2 * step - (chunks - 1))

    odd = lax.rem(s, 2)
    part_cols = (
        pl.ds(1 + (cols - 1) * odd, 1), pl.ds(cols - (cols - 1) * odd, 1), pl.ds(2, cols - 2),
    )
    part_cols_in = (
        pl.ds((cols - 1) * odd, 1), pl.ds(cols - 1 - (cols - 1) * odd, 1), pl.ds(1, cols - 2),
    )

    def z_copy(layer, side, part, block):
        ks = rows_of(block)
        if layer == 0:
            src = x_ref.at[:, 0 if side == 0 else rows - 1, part_cols_in[part], ks]
        else:
            src = buf1.at[:, 1 if side == 0 else rows, part_cols[part], ks]
        return pltpu.make_async_remote_copy(
            src_ref=src,
            dst_ref=bufs[layer].at[:, rows + 1 if side == 0 else 0, part_cols[part], ks],
            send_sem=z_send.at[layer, side, part, block],
            recv_sem=z_recv.at[layer, side, part, block],
            device_id=down if side == 0 else up,
            device_id_type=MESH,
        )

    def j_copy(layer, side, block):
        ks = rows_of(block)
        if layer == 0:
            src = x_ref.at[:, :, 0 if side == 0 else cols - 1, ks]
        else:
            src = buf1.at[:, 1 : rows + 1, 1 if side == 0 else cols, ks]
        return pltpu.make_async_remote_copy(
            src_ref=src,
            dst_ref=bufs[layer].at[:, 1 : rows + 1, cols + 1 if side == 0 else 0, ks],
            send_sem=j_send.at[layer, side, block],
            recv_sem=j_recv.at[layer, side, block],
            device_id=left if side == 0 else right,
            device_id_type=MESH,
        )

    far_side = {"scol": lax.rem(s + n_col - 1 + 2 * odd, n_col)}
    near_side = {"scol": lax.rem(s + n_col + 1 - 2 * odd, n_col)}

    def c_copy(layer, part, end, block):
        ks = rows_of(block)
        row = 0 if end == 0 else rows + 1
        to_right = odd if part == FAR else 1 - odd
        return pltpu.make_async_remote_copy(
            src_ref=bufs[layer].at[:, row, 1 + (cols - 1) * to_right, ks],
            dst_ref=bufs[layer].at[:, row, (cols + 1) * (1 - to_right), ks],
            send_sem=c_send.at[layer, part, end, block],
            recv_sem=c_recv.at[layer, part, end, block],
            device_id=far_side if part == FAR else near_side,
            device_id_type=MESH,
        )

    def e_copy(layer):
        return pltpu.make_async_remote_copy(
            src_ref=edge_out.at[layer],
            dst_ref=edge_in.at[layer],
            send_sem=e_send.at[layer],
            recv_sem=e_recv.at[layer],
            device_id=across,
            device_id_type=MESH,
        )

    z_sides = ((0, has_down, has_up), (1, has_up, has_down))
    j_sides = ((0, has_left, has_right), (1, has_right, has_left))
    ends = ((0, has_down), (1, has_up))
    has_far = (has_right & (odd == 1)) | (has_left & (odd == 0))
    has_near = (has_right & (odd == 0)) | (has_left & (odd == 1))
    beside = (has_far, has_near)

    first, last = lax.rem(r, Z_RING) == 0, lax.rem(r, Z_RING) == Z_RING - 1
    up_later, down_later = has_up & jnp.logical_not(last), has_down & first
    up_earlier, down_earlier = has_up & last, has_down & jnp.logical_not(first)
    later = ((up_later, up), (down_later, down), (has_right, right), (t == 0, across))
    earlier = (
        (up_earlier, up, 1), (down_earlier, down, 0), (has_left, left, 2), (t == 1, across, 3),
    )
    barrier = pltpu.get_barrier_semaphore()
    for present, device in later:
        @pl.when(present)
        def _():
            pl.semaphore_signal(barrier, inc=1, device_id=device, device_id_type=MESH)

    awaited = sum(present.astype(jnp.int32) for present, _, _ in earlier)

    @pl.when(awaited > 0)
    def _():
        pl.semaphore_wait(barrier, awaited)

    for present, device, slot in earlier:
        @pl.when(present)
        def _():
            pl.semaphore_signal(hello.at[slot], inc=1, device_id=device, device_id_type=MESH)

    def send_rows(layer, side, items):
        for part, step in items:
            z_copy(layer, side, part, order(step)).start()

    def send_cols(layer, side, items):
        for part, step in items:
            if part == FAR:
                j_copy(layer, side, order(step)).start()

    def send_items(layer, items):
        for side, sends, _ in z_sides:
            @pl.when(sends)
            def _():
                send_rows(layer, side, items)

        for side, sends, _ in j_sides:
            @pl.when(sends)
            def _():
                send_cols(layer, side, items)

    def send_first(send, side, present, slot=None):
        @pl.when(present)
        def _():
            if slot is not None:
                pl.semaphore_wait(hello.at[slot], 1)
            send(0, side, ORDERS[0])

    send_first(send_rows, 0, down_earlier)
    send_first(send_rows, 1, up_earlier)
    send_first(send_cols, 0, has_left)

    local = pltpu.make_async_copy(x_ref, buf0.at[:, 1 : rows + 1, 1 : cols + 1], in_sem.at[0])
    small = [
        pltpu.make_async_copy(ws_hbm, ws_ref, in_sem.at[1]),
        pltpu.make_async_copy(wt_hbm, wt_ref, in_sem.at[2]),
        pltpu.make_async_copy(bias_hbm, bias_ref, in_sem.at[3]),
    ]
    for copy in small:
        copy.start()
    local.start()
    send_first(send_rows, 1, up_later, 0)
    send_first(send_rows, 0, down_later, 1)
    send_first(send_cols, 1, has_right, 2)

    @pl.when(t == 0)
    def _():
        pl.semaphore_wait(hello.at[3], 1)

    for buf in bufs:
        for row, present in ((0, has_down), (rows + 1, has_up)):
            @pl.when(jnp.logical_not(present))
            def _():
                buf[:, row] = jnp.zeros((channels, cols + 2, depth, width), BF16)

        for col, present in ((0, has_left), (cols + 1, has_right)):
            @pl.when(jnp.logical_not(present))
            def _():
                buf[:, :, col] = jnp.zeros((channels, rows + 2, depth, width), BF16)

    for copy in small:
        copy.wait()
    for layer in range(2):
        build_weights(layer, ws_ref, wt_ref, src_mat, tgt_mat)
        spare = jnp.zeros((channels, rows, cols, PAD, width), F32)
        sums[layer][:, :, :, 0:PAD] = spare
        sums[layer][:, :, :, depth + PAD : depth + 2 * PAD] = spare
        for channel in range(channels):
            sums[layer][channel, :, :, PAD : depth + PAD] = jnp.full(
                (rows, cols, depth, width), bias_ref[layer, channel], F32
            )

    lane = iota((channels * STEP, width), 1)

    def target_pass(layer, block):
        buf, total = bufs[layer], sums[layer]
        ks = rows_of(block)
        base = pl.multiple_of(block * STEP, STEP)
        for i in range(rows):
            for pair in range(cols // 2):
                shifted = [[], [], []]
                for n in range(2):
                    tile = buf[:, i + 1, 1 + 2 * pair + n, ks].reshape(channels * STEP, width)
                    wide = tile.astype(F32)
                    before = jnp.where(lane == 0, 0.0, pltpu.roll(wide, 1, 1))
                    after = jnp.where(lane == width - 1, 0.0, pltpu.roll(wide, width - 1, 1))
                    for second, piece in enumerate((before.astype(BF16), tile, after.astype(BF16))):
                        shifted[second].append(piece)
                stack = jnp.concatenate([jnp.concatenate(p, axis=1) for p in shifted], axis=0)
                got = jnp.dot(tgt_mat[layer], stack, preferred_element_type=F32)
                for n in range(2):
                    j = 2 * pair + n
                    part = got[:, width * n : width * n + width]
                    total[:, i, j, pl.ds(base + PAD, STEP)] += part[0:128].reshape(channels, STEP, width)
                    total[:, i, j, pl.ds(base + PAD + STEP, PAD)] += part[128:192].reshape(channels, PAD, width)
                    total[:, i, j, pl.ds(base, PAD)] += part[192:256].reshape(channels, PAD, width)

    def edge_start(layer):
        for half, place in ((0, depth + PAD), (1, PAD - 1)):
            @pl.when(t == half)
            def _():
                for i in range(rows):
                    for j in range(cols):
                        edge_out[layer, i, j] = sums[layer][:, i, j, place]

        e_copy(layer).start()

    def edge_add(layer):
        e_copy(layer).wait_recv()
        for half, place in ((0, depth + PAD - 1), (1, PAD)):
            @pl.when(t == half)
            def _():
                for i in range(rows):
                    for j in range(cols):
                        sums[layer][:, i, j, place] += edge_in[layer, i, j]

    def stack_of(layer, ks, pair, source_rows):
        buf = bufs[layer]
        parts = []
        for a in source_rows:
            tiles = [buf[:, a, 2 * pair + b, ks].reshape(channels * STEP, width) for b in range(4)]
            parts += [jnp.concatenate([tiles[b], tiles[b + 1]], axis=1) for b in range(3)]
        return jnp.concatenate(parts, axis=0)

    def sums_at(layer, i, j, block):
        base = pl.multiple_of(block * STEP, STEP)
        return sums[layer].at[:, i, j, pl.ds(base + PAD, STEP)]

    def own_rows_pass(layer, block):
        for pair in range(cols // 2):
            stack = stack_of(layer, rows_of(block), pair, (1, 2))
            got = jnp.dot(src_mat[layer, :, 384:1152], stack, preferred_element_type=F32)
            for i in range(rows):
                for n in range(2):
                    part = got[128 * i : 128 * i + 128, width * n : width * n + width]
                    sums_at(layer, i, 2 * pair + n, block)[...] += part.reshape(channels, STEP, width)

    def finish(layer, block):
        ks = rows_of(block)
        for pair in range(cols // 2):
            for i in range(rows):
                stack = stack_of(layer, ks, pair, (3 * i,))
                mat = src_mat[layer, 128 * i : 128 * i + 128, 1152 * i : 1152 * i + 384]
                got = jnp.dot(mat, stack, preferred_element_type=F32)
                for n in range(2):
                    j = 2 * pair + n
                    part = got[:, width * n : width * n + width].reshape(channels, STEP, width)
                    part = part + sums_at(layer, i, j, block)[...]
                    center = bufs[layer][:, i + 1, j + 1, ks].astype(F32)
                    value = (center + jnp.maximum(part, 0.0)).astype(BF16)
                    if layer == 0:
                        buf1[:, i + 1, j + 1, ks] = value
                    else:
                        out_ref[:, i, j, ks] = value

    local.wait()

    @pl.loop(0, chunks)
    def _(step):
        target_pass(0, order(step))

        @pl.when(step == 0)
        def _():
            edge_start(0)

    def wait_sends():
        @pl.loop(0, chunks)
        def _(block):
            for layer in range(2):
                for side, sends, _ in z_sides:
                    @pl.when(sends)
                    def _():
                        for part in range(3):
                            z_copy(layer, side, part, block).wait_send()

                for side, sends, _ in j_sides:
                    @pl.when(sends)
                    def _():
                        j_copy(layer, side, block).wait_send()

                for part in (FAR, NEAR):
                    for end, present in ends:
                        @pl.when(beside[part] & present)
                        def _():
                            c_copy(layer, part, end, block).wait_send()

        for layer in range(2):
            e_copy(layer).wait_send()

    def take_outer(layer, part, step):
        block = order(step)
        for end, present in ends:
            @pl.when(present)
            def _():
                z_copy(layer, 1 - end, part, block).wait_recv()

                @pl.when(beside[part])
                def _():
                    c_copy(layer, part, end, block).start()

    def take_cols(layer, step):
        block = order(step)
        for side, _, receives in j_sides:
            @pl.when(receives)
            def _():
                j_copy(layer, side, block).wait_recv()

        own_rows_pass(layer, block)

    def take_inner(layer, step):
        block = order(step)
        for part in (FAR, NEAR):
            for end, present in ends:
                @pl.when(beside[part] & present)
                def _():
                    c_copy(layer, part, end, block).wait_recv()

        for end, present in ends:
            @pl.when(present)
            def _():
                z_copy(layer, 1 - end, INNER, block).wait_recv()

        finish(layer, block)

    unsent = list(ORDERS[1])
    for layer in range(2):
        for part, step in ORDERS[layer]:
            if part != INNER:
                take_outer(layer, part, step)
                if part == NEAR:
                    take_cols(layer, step)
                continue
            if step == 0:
                edge_add(layer)
            if layer == 1 and step == chunks - 1:
                wait_sends()
            take_inner(layer, step)
            if layer == 1:
                continue
            ready = []
            while unsent and unsent[0][1] <= step:
                ready.append(unsent.pop(0))
            send_items(1, ready)
            target_pass(1, order(step))
            if step == 0:
                edge_start(1)


def by_channels(weight):
    return jnp.transpose(weight, (0, 2, 3, 1)).reshape(-1, weight.shape[1])


def shards(sizes, volume, src_weight, tgt_weight, bias):
    channels, rows, cols, depth, width = volume.shape
    chunks = depth // STEP
    padded = pltpu.VMEM((channels, rows + 2, cols + 2, depth, width), BF16)
    total = pltpu.VMEM((channels, rows, cols, depth + 2 * PAD, width), F32)
    edges = pltpu.VMEM((2, rows, cols, channels, width), F32)
    dma = pltpu.SemaphoreType.DMA
    operands = (volume, by_channels(src_weight), by_channels(tgt_weight), bias)
    return pl.pallas_call(
        functools.partial(kernel, sizes),
        out_shape=jax.ShapeDtypeStruct(volume.shape, BF16),
        in_specs=[
            pl.BlockSpec(memory_space=pltpu.HBM),
            pl.BlockSpec(memory_space=pltpu.HBM),
            pl.BlockSpec(memory_space=pltpu.HBM),
            pl.BlockSpec(memory_space=pltpu.HBM),
        ],
        out_specs=pl.BlockSpec(memory_space=pltpu.VMEM),
        scratch_shapes=[
            pltpu.VMEM((2 * channels * channels, 9), BF16),
            pltpu.VMEM((2 * channels * channels, 9), BF16),
            pltpu.SMEM((2, channels), F32),
            padded, padded, total, total,
            pltpu.VMEM((2, 256, 12 * 128), BF16),
            pltpu.VMEM((2, 256, 3 * 128), BF16),
            edges, edges,
            dma((2, 2, 3, chunks)), dma((2, 2, 3, chunks)),
            dma((2, 2, chunks)), dma((2, 2, chunks)),
            dma((2, 2, 2, chunks)), dma((2, 2, 2, chunks)),
            dma((2,)), dma((2,)),
            dma((4,)),
            pltpu.SemaphoreType.REGULAR((4,)),
        ],
        compiler_params=pltpu.CompilerParams(
            collective_id=0, has_side_effects=True, vmem_limit_bytes=40 * 1024 * 1024
        ),
    )(*(pltpu.with_memory_space_constraint(v, pltpu.HBM) for v in operands))


def solution(mesh):
    sizes = (mesh.shape["srow"], mesh.shape["scol"])
    return jax.shard_map(
        functools.partial(shards, sizes),
        mesh=mesh,
        in_specs=(P(None, "srow", "scol", "trow", None), P(), P(), P()),
        out_specs=P(None, "srow", "scol", "trow", None),
        check_vma=False,
    )
```
